256 devices in a mesh: row: 32 (over z, y), col: 8 (over x, core).
Axes of the slice: x: 4, y: 4, z: 8, core: 2. Of those that a mesh axis runs over, the one named last changes fastest.
Arguments:
- features: bfloat16 [96, 256, 2048], P(None, 'row', 'col'), may hold values from -6 to 6
- cotangent: bfloat16 [96, 256, 2048], P(None, 'row', 'col'), may hold values from -6 to 6
- weight_one: bfloat16 [3, 3, 96, 96], replicated, may hold values from -0.21875 to 0.21875
- bias_one: float32 [96], replicated, may hold values from -3 to 3
- weight_two: bfloat16 [3, 3, 96, 96], replicated, may hold values from -0.21875 to 0.21875
Outputs:
- input_grad: bfloat16 [96, 256, 2048], P(None, 'row', 'col')
- grad_one: float32 [82944], P(('row', 'col'))
- grad_two: float32 [82944], P(('row', 'col'))
The draws below stay inside these ranges and needn't reach their ends.
All inputs are finite; a program needn't handle non-finite values.
Results may differ from the reference program's by a relative error of at most 0.0032.
Values may be sent and summed in bfloat16 or wider, within the bound.
A program may use at most 64 MiB of HBM per device.

```python
import jax
import jax.numpy as jnp
from jax import lax

C = 96
NH = 256
NW = 2048


def level_of(rng, dims, pieces, low, high):
    loudness = 1.0
    for position, blocks in pieces:
        heights = jax.random.uniform(jax.random.fold_in(jax.random.fold_in(rng, 6), position), (blocks,), jnp.float32, low / len(pieces), high / len(pieces))
        loudness = loudness * jnp.repeat(jnp.exp(heights), dims[position] // blocks).reshape((-1,) + (1,) * (len(dims) - 1 - position))
    return loudness


def bell_draw(stream_key, shape, deviation, limit, shards=(), kind=jnp.bfloat16):
    entries = deviation * jax.random.normal(stream_key, shape, jnp.float32)
    if shards:
        entries = entries * level_of(stream_key, shape, shards, -0.22, 0.18)
    return jnp.clip(entries, -limit, limit).astype(kind)


def setup_inputs(seed: int = 0) -> dict:
    arg_keys = jax.random.split(jax.random.key(seed), 6)
    return {
        "features": bell_draw(arg_keys[0], (C, NH, NW), 1.0, 6.0, ((1, 32), (2, 8))),
        "cotangent": bell_draw(arg_keys[1], (C, NH, NW), 1.0, 6.0, ((1, 32), (2, 8))),
        "weight_one": bell_draw(arg_keys[2], (3, 3, C, C), (9 * C) ** -0.5, 0.21875),
        "bias_one": bell_draw(arg_keys[3], (C,), 0.5, 3.0, (), jnp.float32),
        "weight_two": bell_draw(arg_keys[4], (3, 3, C, C), (9 * C) ** -0.5, 0.21875),
    }


def conv(field, kernel):
    taps = jnp.transpose(kernel, (2, 3, 0, 1))
    return lax.conv_general_dilated(field[None], taps, (1, 1), ((1, 1), (1, 1)), precision=lax.Precision.HIGHEST)[0]

def tconv(field, kernel):
    taps = jnp.transpose(kernel[::-1, ::-1], (3, 2, 0, 1))
    return lax.conv_general_dilated(field[None], taps, (1, 1), ((1, 1), (1, 1)), precision=lax.Precision.HIGHEST)[0]

def kernel_grad(upper, lower):
    channels, height, breadth = lower.shape
    padded = jnp.pad(lower, ((0, 0), (1, 1), (1, 1)))
    flat_upper = upper.reshape(channels, -1)
    parts = []
    for offset_y in range(3):
        for offset_x in range(3):
            moved = padded[:, offset_y:offset_y + height, offset_x:offset_x + breadth].reshape(channels, -1)
            parts.append(jnp.dot(flat_upper, moved.T, precision=lax.Precision.HIGHEST))
    return jnp.stack(parts)

def reference(features, cotangent, weight_one, bias_one, weight_two):
    scale = float(NH * NW) ** (-0.5)
    feat32 = features.astype(jnp.float32)
    cot32 = cotangent.astype(jnp.float32)
    hidden = conv(feat32, weight_one.astype(jnp.float32)) + bias_one[:, None, None]
    act = jax.nn.silu(hidden).astype(jnp.bfloat16)
    act_grad = tconv(cot32, weight_two.astype(jnp.float32))
    sig = jax.nn.sigmoid(hidden)
    hidden_grad = (act_grad * sig * (1.0 + hidden * (1.0 - sig))).astype(jnp.bfloat16)
    input_grad = (cot32 + tconv(hidden_grad.astype(jnp.float32), weight_one.astype(jnp.float32))).astype(jnp.bfloat16)
    grad_two = (kernel_grad(cot32, act.astype(jnp.float32)) * scale).reshape(-1)
    grad_one = (kernel_grad(hidden_grad.astype(jnp.float32), feat32) * scale).reshape(-1)
    return (input_grad, grad_one, grad_two)
```

```python
import jax
import jax.numpy as jnp
from jax import lax
from jax.sharding import PartitionSpec as P


def padded_2(cells, sides, width):
    for axis, dim in sides:
        count = lax.axis_size(axis)
        ends = count - 1
        head = lax.slice_in_dim(cells, 0, width, axis=dim)
        tail = lax.slice_in_dim(cells, cells.shape[dim] - width, cells.shape[dim], axis=dim)
        cells = jnp.concatenate(
            [
                lax.ppermute(tail, axis, [(i, (i + 1) % count) for i in range(ends)]),
                cells,
                lax.ppermute(head, axis, [((i + 1) % count, i) for i in range(ends)]),
            ],
            axis=dim,
        )
    return cells


def window(padded, start_y, start_x, tile_rows, tile_cols):
    channels = padded.shape[0]
    piece = lax.slice(
        padded, (0, start_y, start_x), (channels, start_y + tile_rows, start_x + tile_cols)
    )
    return piece.reshape(channels, tile_rows * tile_cols)


def backward_taps(padded, kernel, other, tile_rows, tile_cols):
    channels = padded.shape[0]
    total = jnp.zeros((channels, tile_rows * tile_cols), jnp.float32)
    grads = []
    for offset_y in range(3):
        for offset_x in range(3):
            patch = window(padded, 2 - offset_y, 2 - offset_x, tile_rows, tile_cols)
            total = total + lax.dot_general(
                kernel[offset_y, offset_x],
                patch,
                (((0,), (0,)), ((), ())),
                preferred_element_type=jnp.float32,
            )
            grads.append(
                lax.dot_general(
                    patch, other, (((1,), (1,)), ((), ())), preferred_element_type=jnp.float32
                )
            )
    return (total, jnp.stack(grads).reshape(-1))


def reduce_weights(grads):
    shards = lax.axis_size("row") * lax.axis_size("col")
    stacked = jnp.stack(grads).reshape(len(grads), shards, -1)
    spread = lax.all_to_all(stacked, ("row", "col"), 1, 1, tiled=True)
    summed = spread.sum(axis=1)
    return (summed[0], summed[1])


def local(features, cotangent, weight_one, bias_one, weight_two):
    channels, tile_rows, tile_cols = features.shape
    cell_count = tile_rows * tile_cols
    scale = float(cell_count * lax.axis_size("row") * lax.axis_size("col")) ** (-0.5)
    padded_input = padded_2(features, (("row", 1), ("col", 2)), 1)
    padded_cot = padded_2(cotangent, (("row", 1), ("col", 2)), 1)
    hidden = jnp.zeros((channels, cell_count), jnp.float32)
    for offset_y in range(3):
        for offset_x in range(3):
            patch = window(padded_input, offset_y, offset_x, tile_rows, tile_cols)
            hidden = hidden + jnp.dot(
                weight_one[offset_y, offset_x], patch, preferred_element_type=jnp.float32
            )
    hidden = hidden + bias_one[:, None]
    act = jax.nn.silu(hidden).astype(jnp.bfloat16)
    act_grad, grad_two = backward_taps(padded_cot, weight_two, act, tile_rows, tile_cols)
    grad_two = grad_two * scale
    sig = jax.nn.sigmoid(hidden)
    hidden_grad = (act_grad * sig * (1.0 + hidden * (1.0 - sig))).astype(jnp.bfloat16)
    padded_hid = padded_2(
        hidden_grad.reshape(channels, tile_rows, tile_cols), (("row", 1), ("col", 2)), 1
    )
    back_input, grad_one = backward_taps(
        padded_hid, weight_one, features.reshape(channels, cell_count), tile_rows, tile_cols
    )
    grad_one = grad_one * scale
    input_grad = (cotangent.reshape(channels, cell_count).astype(jnp.float32) + back_input).astype(
        jnp.bfloat16
    )
    input_grad = input_grad.reshape(channels, tile_rows, tile_cols)
    summed_one, summed_two = reduce_weights((grad_one, grad_two))
    return (input_grad, summed_one, summed_two)


def solution(mesh):
    placed = (P(None, "row", "col"), P(None, "row", "col"), P(), P(), P())
    return jax.shard_map(
        local,
        mesh=mesh,
        in_specs=placed,
        out_specs=(P(None, "row", "col"), P(("row", "col")), P(("row", "col"))),
        check_vma=False,
    )
```

```python
import jax
import jax.numpy as jnp
from jax import lax
from jax.sharding import PartitionSpec as P


def padded_2(cells, sides, width):
    for axis, dim in sides:
        count = lax.axis_size(axis)
        ends = count - 1
        head = lax.slice_in_dim(cells, 0, width, axis=dim)
        tail = lax.slice_in_dim(cells, cells.shape[dim] - width, cells.shape[dim], axis=dim)
        cells = jnp.concatenate(
            [
                lax.ppermute(tail, axis, [(i, (i + 1) % count) for i in range(ends)]),
                cells,
                lax.ppermute(head, axis, [((i + 1) % count, i) for i in range(ends)]),
            ],
            axis=dim,
        )
    return cells


def window(padded, start_y, start_x, tile_rows, tile_cols):
    channels = padded.shape[0]
    piece = lax.slice(
        padded, (0, start_y, start_x), (channels, start_y + tile_rows, start_x + tile_cols)
    )
    return piece.reshape(channels, tile_rows * tile_cols)


def conv_valid(cells, taps):
    return lax.conv_general_dilated(
        cells[None], taps, (1, 1), "VALID", preferred_element_type=jnp.float32
    )[0]


def forward_taps(kernel):
    return jnp.transpose(kernel, (2, 3, 0, 1))


def backward_taps(kernel):
    return jnp.transpose(kernel[::-1, ::-1], (3, 2, 0, 1))


def kernel_grads(upper, padded, start, tile_rows, tile_cols):
    grads = []
    for offset_y in range(3):
        for offset_x in range(3):
            patch = window(padded, start + offset_y, start + offset_x, tile_rows, tile_cols)
            grads.append(
                lax.dot_general(
                    upper, patch, (((1,), (1,)), ((), ())), preferred_element_type=jnp.float32
                )
            )
    return jnp.stack(grads).reshape(-1)


def reduce_weights(grads):
    shards = lax.axis_size("row") * lax.axis_size("col")
    stacked = jnp.stack(grads).reshape(len(grads), shards, -1)
    spread = lax.all_to_all(stacked, ("row", "col"), 1, 1, tiled=True)
    summed = spread.sum(axis=1)
    return (summed[0], summed[1])


def local(features, cotangent, weight_one, bias_one, weight_two):
    channels, tile_rows, tile_cols = features.shape
    row_count, col_count = lax.axis_size("row"), lax.axis_size("col")
    scale = float(tile_rows * tile_cols * row_count * col_count) ** (-0.5)
    both = padded_2(
        jnp.concatenate([features, cotangent], axis=0), (("row", 1), ("col", 2)), 2
    )
    padded_input, padded_cot = both[:channels], both[channels:]
    grid_row = (
        lax.axis_index("row") * tile_rows - 1
        + lax.broadcasted_iota(jnp.int32, (tile_rows + 2, 1), 0)
    )
    grid_col = (
        lax.axis_index("col") * tile_cols - 1
        + lax.broadcasted_iota(jnp.int32, (1, tile_cols + 2), 1)
    )
    inside = (
        (grid_row >= 0)
        & (grid_row < row_count * tile_rows)
        & (grid_col >= 0)
        & (grid_col < col_count * tile_cols)
    )
    hidden = conv_valid(padded_input, forward_taps(weight_one)) + bias_one[:, None, None]
    act = jnp.where(inside, jax.nn.silu(hidden), 0.0).astype(jnp.bfloat16)
    act_grad = conv_valid(padded_cot, backward_taps(weight_two))
    sig = jax.nn.sigmoid(hidden)
    hidden_grad = jnp.where(
        inside, act_grad * sig * (1.0 + hidden * (1.0 - sig)), 0.0
    ).astype(jnp.bfloat16)
    back_input = conv_valid(hidden_grad, backward_taps(weight_one))
    input_grad = (cotangent.astype(jnp.float32) + back_input).astype(jnp.bfloat16)
    grad_two = kernel_grads(
        cotangent.reshape(channels, -1), act, 0, tile_rows, tile_cols
    ) * scale
    inner_grad = hidden_grad[:, 1 : 1 + tile_rows, 1 : 1 + tile_cols].reshape(channels, -1)
    grad_one = kernel_grads(inner_grad, padded_input, 1, tile_rows, tile_cols) * scale
    summed_one, summed_two = reduce_weights((grad_one, grad_two))
    return (input_grad, summed_one, summed_two)


def solution(mesh):
    placed = (P(None, "row", "col"), P(None, "row", "col"), P(), P(), P())
    return jax.shard_map(
        local,
        mesh=mesh,
        in_specs=placed,
        out_specs=(P(None, "row", "col"), P(("row", "col")), P(("row", "col"))),
        check_vma=False,
    )
```

```python
import jax
import jax.numpy as jnp
from jax import lax
from jax.sharding import PartitionSpec as P


def padded_2(cells, sides, width):
    for axis, dim in sides:
        count = lax.axis_size(axis)
        ends = count - 1
        head = lax.slice_in_dim(cells, 0, width, axis=dim)
        tail = lax.slice_in_dim(cells, cells.shape[dim] - width, cells.shape[dim], axis=dim)
        cells = jnp.concatenate(
            [
                lax.ppermute(tail, axis, [(i, (i + 1) % count) for i in range(ends)]),
                cells,
                lax.ppermute(head, axis, [((i + 1) % count, i) for i in range(ends)]),
            ],
            axis=dim,
        )
    return cells


def window(padded, start_y, start_x, tile_rows, tile_cols):
    channels = padded.shape[0]
    piece = lax.slice(
        padded, (0, start_y, start_x), (channels, start_y + tile_rows, start_x + tile_cols)
    )
    return piece.reshape(channels, tile_rows * tile_cols)


def conv_taps(padded, kernel, flip, rows, cols):
    channels = padded.shape[0]
    total = jnp.zeros((kernel.shape[2], rows * cols), jnp.float32)
    for offset_y in range(3):
        for offset_x in range(3):
            if flip:
                patch = window(padded, 2 - offset_y, 2 - offset_x, rows, cols)
                taps, contract = kernel[offset_y, offset_x], 0
            else:
                patch = window(padded, offset_y, offset_x, rows, cols)
                taps, contract = kernel[offset_y, offset_x], 1
            total = total + lax.dot_general(
                taps, patch, (((contract,), (0,)), ((), ())), preferred_element_type=jnp.float32
            )
    return total


def kernel_grads(upper, padded, start, tile_rows, tile_cols):
    grads = []
    for offset_y in range(3):
        for offset_x in range(3):
            patch = window(padded, start + offset_y, start + offset_x, tile_rows, tile_cols)
            grads.append(
                lax.dot_general(
                    upper, patch, (((1,), (1,)), ((), ())), preferred_element_type=jnp.float32
                )
            )
    return jnp.stack(grads).reshape(-1)


def reduce_weights(grads):
    shards = lax.axis_size("row") * lax.axis_size("col")
    stacked = jnp.stack(grads).reshape(len(grads), shards, -1)
    spread = lax.all_to_all(stacked, ("row", "col"), 1, 1, tiled=True)
    summed = spread.sum(axis=1)
    return (summed[0], summed[1])


def local(features, cotangent, weight_one, bias_one, weight_two):
    channels, tile_rows, tile_cols = features.shape
    row_count, col_count = lax.axis_size("row"), lax.axis_size("col")
    scale = float(tile_rows * tile_cols * row_count * col_count) ** (-0.5)
    both = padded_2(
        jnp.concatenate([features, cotangent], axis=0), (("row", 1), ("col", 2)), 2
    )
    padded_input, padded_cot = both[:channels], both[channels:]
    grid_row = (
        lax.axis_index("row") * tile_rows - 1
        + lax.broadcasted_iota(jnp.int32, (tile_rows + 2, 1), 0)
    )
    grid_col = (
        lax.axis_index("col") * tile_cols - 1
        + lax.broadcasted_iota(jnp.int32, (1, tile_cols + 2), 1)
    )
    inside = (
        (grid_row >= 0)
        & (grid_row < row_count * tile_rows)
        & (grid_col >= 0)
        & (grid_col < col_count * tile_cols)
    )
    ext_rows, ext_cols = tile_rows + 2, tile_cols + 2
    inside = inside.reshape(1, ext_rows * ext_cols)
    hidden = conv_taps(padded_input, weight_one, False, ext_rows, ext_cols) + bias_one[:, None]
    act = jnp.where(inside, jax.nn.silu(hidden), 0.0).astype(jnp.bfloat16)
    act_grad = conv_taps(padded_cot, weight_two, True, ext_rows, ext_cols)
    sig = jax.nn.sigmoid(hidden)
    hidden_grad = jnp.where(
        inside, act_grad * sig * (1.0 + hidden * (1.0 - sig)), 0.0
    ).astype(jnp.bfloat16)
    act = act.reshape(channels, ext_rows, ext_cols)
    hidden_grad = hidden_grad.reshape(channels, ext_rows, ext_cols)
    back_input = conv_taps(hidden_grad, weight_one, True, tile_rows, tile_cols)
    input_grad = (cotangent.reshape(channels, -1).astype(jnp.float32) + back_input).astype(
        jnp.bfloat16
    ).reshape(channels, tile_rows, tile_cols)
    grad_two = kernel_grads(
        cotangent.reshape(channels, -1), act, 0, tile_rows, tile_cols
    ) * scale
    inner_grad = window(hidden_grad, 1, 1, tile_rows, tile_cols)
    grad_one = kernel_grads(inner_grad, padded_input, 1, tile_rows, tile_cols) * scale
    summed_one, summed_two = reduce_weights((grad_one, grad_two))
    return (input_grad, summed_one, summed_two)


def solution(mesh):
    placed = (P(None, "row", "col"), P(None, "row", "col"), P(), P(), P())
    return jax.shard_map(
        local,
        mesh=mesh,
        in_specs=placed,
        out_specs=(P(None, "row", "col"), P(("row", "col")), P(("row", "col"))),
        check_vma=False,
    )
```

```python
import jax
import jax.numpy as jnp
from jax import lax
from jax.sharding import PartitionSpec as P


def padded_2(cells, sides, width):
    for axis, dim in sides:
        count = lax.axis_size(axis)
        ends = count - 1
        head = lax.slice_in_dim(cells, 0, width, axis=dim)
        tail = lax.slice_in_dim(cells, cells.shape[dim] - width, cells.shape[dim], axis=dim)
        cells = jnp.concatenate(
            [
                lax.ppermute(tail, axis, [(i, (i + 1) % count) for i in range(ends)]),
                cells,
                lax.ppermute(head, axis, [((i + 1) % count, i) for i in range(ends)]),
            ],
            axis=dim,
        )
    return cells


def window(padded, start_y, start_x, tile_rows, tile_cols):
    channels = padded.shape[0]
    piece = lax.slice(
        padded, (0, start_y, start_x), (channels, start_y + tile_rows, start_x + tile_cols)
    )
    return piece.reshape(channels, tile_rows * tile_cols)


def conv_taps(padded, kernel, flip, rows, cols):
    total = jnp.zeros((kernel.shape[2], rows * cols), jnp.float32)
    for offset_y in range(3):
        for offset_x in range(3):
            if flip:
                patch = window(padded, 2 - offset_y, 2 - offset_x, rows, cols)
            else:
                patch = window(padded, offset_y, offset_x, rows, cols)
            total = total + lax.dot_general(
                kernel[offset_y, offset_x],
                patch,
                (((0 if flip else 1,), (0,)), ((), ())),
                preferred_element_type=jnp.float32,
            )
    return total


def kernel_grads(pairs):
    return jnp.stack(
        [
            lax.dot_general(
                upper, lower, (((1,), (1,)), ((), ())), preferred_element_type=jnp.float32
            )
            for upper, lower in pairs
        ]
    ).reshape(-1)


def reduce_weights(grads):
    shards = lax.axis_size("row") * lax.axis_size("col")
    stacked = jnp.stack(grads).reshape(len(grads), shards, -1)
    spread = lax.all_to_all(stacked, ("row", "col"), 1, 1, tiled=True)
    summed = spread.sum(axis=1)
    return (summed[0], summed[1])


def local(features, cotangent, weight_one, bias_one, weight_two):
    channels, tile_rows, tile_cols = features.shape
    row_count, col_count = lax.axis_size("row"), lax.axis_size("col")
    scale = float(tile_rows * tile_cols * row_count * col_count) ** (-0.5)
    ext_rows = tile_rows + 2
    both = padded_2(jnp.concatenate([features, cotangent], axis=0), (("row", 1),), 2)
    both = padded_2(both, (("col", 2),), 1)
    padded_input, padded_cot = both[:channels], both[channels:]
    grid_row = (
        lax.axis_index("row") * tile_rows
        - 1
        + lax.broadcasted_iota(jnp.int32, (1, ext_rows * tile_cols), 1) // tile_cols
    )
    inside = (grid_row >= 0) & (grid_row < row_count * tile_rows)
    inner = slice(tile_cols, tile_cols * (tile_rows + 1))
    hidden = conv_taps(padded_input, weight_one, False, ext_rows, tile_cols) + bias_one[:, None]
    act = jax.nn.silu(hidden[:, inner]).astype(jnp.bfloat16)
    act_grad = conv_taps(padded_cot, weight_two, True, ext_rows, tile_cols)
    sig = jax.nn.sigmoid(hidden)
    hidden_grad = jnp.where(
        inside, act_grad * sig * (1.0 + hidden * (1.0 - sig)), 0.0
    ).astype(jnp.bfloat16)
    padded_hid = padded_2(
        hidden_grad.reshape(channels, ext_rows, tile_cols), (("col", 2),), 1
    )
    back_input = conv_taps(padded_hid, weight_one, True, tile_rows, tile_cols)
    input_grad = (cotangent.reshape(channels, -1).astype(jnp.float32) + back_input).astype(
        jnp.bfloat16
    ).reshape(channels, tile_rows, tile_cols)
    grad_two = kernel_grads(
        [
            (window(padded_cot, 3 - offset_y, 2 - offset_x, tile_rows, tile_cols), act)
            for offset_y in range(3)
            for offset_x in range(3)
        ]
    ) * scale
    inner_grad = hidden_grad[:, inner]
    grad_one = kernel_grads(
        [
            (inner_grad, window(padded_input, offset_y + 1, offset_x, tile_rows, tile_cols))
            for offset_y in range(3)
            for offset_x in range(3)
        ]
    ) * scale
    summed_one, summed_two = reduce_weights((grad_one, grad_two))
    return (input_grad, summed_one, summed_two)


def solution(mesh):
    placed = (P(None, "row", "col"), P(None, "row", "col"), P(), P(), P())
    return jax.shard_map(
        local,
        mesh=mesh,
        in_specs=placed,
        out_specs=(P(None, "row", "col"), P(("row", "col")), P(("row", "col"))),
        check_vma=False,
    )
```

```python
import jax
import jax.numpy as jnp
from jax import lax
from jax.sharding import PartitionSpec as P


def padded_2(cells, sides, width):
    for axis, dim in sides:
        count = lax.axis_size(axis)
        ends = count - 1
        head = lax.slice_in_dim(cells, 0, width, axis=dim)
        tail = lax.slice_in_dim(cells, cells.shape[dim] - width, cells.shape[dim], axis=dim)
        cells = jnp.concatenate(
            [
                lax.ppermute(tail, axis, [(i, (i + 1) % count) for i in range(ends)]),
                cells,
                lax.ppermute(head, axis, [((i + 1) % count, i) for i in range(ends)]),
            ],
            axis=dim,
        )
    return cells


def window(padded, start_y, start_x, tile_rows, tile_cols):
    channels = padded.shape[0]
    piece = lax.slice(
        padded, (0, start_y, start_x), (channels, start_y + tile_rows, start_x + tile_cols)
    )
    return piece.reshape(channels, tile_rows * tile_cols)


def backward_taps(padded, kernel, other, tile_rows, tile_cols):
    channels = padded.shape[0]
    total = jnp.zeros((channels, tile_rows * tile_cols), jnp.float32)
    grads = []
    for offset_y in range(3):
        for offset_x in range(3):
            patch = window(padded, 2 - offset_y, 2 - offset_x, tile_rows, tile_cols)
            total = total + lax.dot_general(
                kernel[offset_y, offset_x],
                patch,
                (((0,), (0,)), ((), ())),
                preferred_element_type=jnp.float32,
            )
            grads.append(
                lax.dot_general(
                    patch, other, (((1,), (1,)), ((), ())), preferred_element_type=jnp.float32
                )
            )
    return (total, jnp.stack(grads).reshape(-1))


def reduce_weights(grads):
    rows, cols = lax.axis_size("row"), lax.axis_size("col")
    stacked = jnp.stack(grads).reshape(len(grads), rows, cols, -1)
    stacked = lax.all_to_all(stacked, "col", 2, 2, tiled=True).sum(axis=2)
    summed = lax.all_to_all(stacked, "row", 1, 1, tiled=True).sum(axis=1)
    return (summed[0], summed[1])


def local(features, cotangent, weight_one, bias_one, weight_two):
    channels, tile_rows, tile_cols = features.shape
    cell_count = tile_rows * tile_cols
    scale = float(cell_count * lax.axis_size("row") * lax.axis_size("col")) ** (-0.5)
    padded_both = padded_2(
        jnp.concatenate([features, cotangent], axis=0), (("row", 1), ("col", 2)), 1
    )
    padded_input, padded_cot = padded_both[:channels], padded_both[channels:]
    hidden = jnp.zeros((channels, cell_count), jnp.float32)
    for offset_y in range(3):
        for offset_x in range(3):
            patch = window(padded_input, offset_y, offset_x, tile_rows, tile_cols)
            hidden = hidden + jnp.dot(
                weight_one[offset_y, offset_x], patch, preferred_element_type=jnp.float32
            )
    hidden = hidden + bias_one[:, None]
    act = jax.nn.silu(hidden).astype(jnp.bfloat16)
    act_grad, grad_two = backward_taps(padded_cot, weight_two, act, tile_rows, tile_cols)
    grad_two = grad_two * scale
    sig = jax.nn.sigmoid(hidden)
    hidden_grad = (act_grad * sig * (1.0 + hidden * (1.0 - sig))).astype(jnp.bfloat16)
    padded_hid = padded_2(
        hidden_grad.reshape(channels, tile_rows, tile_cols), (("row", 1), ("col", 2)), 1
    )
    back_input, grad_one = backward_taps(
        padded_hid, weight_one, features.reshape(channels, cell_count), tile_rows, tile_cols
    )
    grad_one = grad_one * scale
    input_grad = (cotangent.reshape(channels, cell_count).astype(jnp.float32) + back_input).astype(
        jnp.bfloat16
    )
    input_grad = input_grad.reshape(channels, tile_rows, tile_cols)
    summed_one, summed_two = reduce_weights((grad_one, grad_two))
    return (input_grad, summed_one, summed_two)


def solution(mesh):
    placed = (P(None, "row", "col"), P(None, "row", "col"), P(), P(), P())
    return jax.shard_map(
        local,
        mesh=mesh,
        in_specs=placed,
        out_specs=(P(None, "row", "col"), P(("row", "col")), P(("row", "col"))),
        check_vma=False,
    )
```

```python
import jax
import jax.numpy as jnp
from jax import lax
from jax.sharding import PartitionSpec as P


def padded_2(cells, sides, width):
    for axis, dim in sides:
        count = lax.axis_size(axis)
        ends = count - 1
        head = lax.slice_in_dim(cells, 0, width, axis=dim)
        tail = lax.slice_in_dim(cells, cells.shape[dim] - width, cells.shape[dim], axis=dim)
        cells = jnp.concatenate(
            [
                lax.ppermute(tail, axis, [(i, (i + 1) % count) for i in range(ends)]),
                cells,
                lax.ppermute(head, axis, [((i + 1) % count, i) for i in range(ends)]),
            ],
            axis=dim,
        )
    return cells


def window(padded, start_y, start_x, tile_rows, tile_cols):
    channels = padded.shape[0]
    piece = lax.slice(
        padded, (0, start_y, start_x), (channels, start_y + tile_rows, start_x + tile_cols)
    )
    return piece.reshape(channels, tile_rows * tile_cols)


def backward_taps(padded, kernel, other, tile_rows, tile_cols):
    channels = padded.shape[0]
    total = jnp.zeros((channels, tile_rows * tile_cols), jnp.float32)
    grads = []
    for offset_y in range(3):
        for offset_x in range(3):
            patch = window(padded, 2 - offset_y, 2 - offset_x, tile_rows, tile_cols)
            total = total + lax.dot_general(
                kernel[offset_y, offset_x],
                patch,
                (((0,), (0,)), ((), ())),
                preferred_element_type=jnp.float32,
            )
            grads.append(
                lax.dot_general(
                    patch, other, (((1,), (1,)), ((), ())), preferred_element_type=jnp.float32
                )
            )
    return (total, jnp.stack(grads).reshape(-1))


def reduce_weights(grads):
    rows, cols = lax.axis_size("row"), lax.axis_size("col")
    stacked = jnp.stack(grads).reshape(len(grads), rows, cols, -1)
    stacked = lax.all_to_all(stacked, "col", 2, 2, tiled=True)
    stacked = stacked.sum(axis=2)
    summed = lax.all_to_all(stacked, "row", 1, 1, tiled=True).sum(axis=1)
    return (summed[0], summed[1])


def block(features, cotangent, weight_one, bias_one, weight_two):
    channels, tile_rows, tile_cols = features.shape
    cell_count = tile_rows * tile_cols
    scale = float(cell_count * lax.axis_size("row") * lax.axis_size("col")) ** (-0.5)
    padded_both = padded_2(
        jnp.concatenate([features, cotangent], axis=0), (("row", 1), ("col", 2)), 1
    )
    padded_input, padded_cot = padded_both[:channels], padded_both[channels:]
    hidden = jnp.zeros((channels, cell_count), jnp.float32)
    for offset_y in range(3):
        for offset_x in range(3):
            patch = window(padded_input, offset_y, offset_x, tile_rows, tile_cols)
            hidden = hidden + jnp.dot(
                weight_one[offset_y, offset_x], patch, preferred_element_type=jnp.float32
            )
    hidden = hidden + bias_one[:, None]
    act = jax.nn.silu(hidden).astype(jnp.bfloat16)
    act_grad, grad_two = backward_taps(padded_cot, weight_two, act, tile_rows, tile_cols)
    grad_two = grad_two * scale
    sig = jax.nn.sigmoid(hidden)
    hidden_grad = (act_grad * sig * (1.0 + hidden * (1.0 - sig))).astype(jnp.bfloat16)
    padded_hid = padded_2(
        hidden_grad.reshape(channels, tile_rows, tile_cols), (("row", 1), ("col", 2)), 1
    )
    inner_grad = hidden_grad.reshape(channels, cell_count)
    grad_one = jnp.stack(
        [
            lax.dot_general(
                inner_grad,
                window(padded_input, offset_y, offset_x, tile_rows, tile_cols),
                (((1,), (1,)), ((), ())),
                preferred_element_type=jnp.float32,
            )
            for offset_y in range(3)
            for offset_x in range(3)
        ]
    ).reshape(-1) * scale
    back_input, _ = backward_taps(padded_hid, weight_one, inner_grad, tile_rows, tile_cols)
    input_grad = (cotangent.reshape(channels, cell_count).astype(jnp.float32) + back_input).astype(
        jnp.bfloat16
    )
    input_grad = input_grad.reshape(channels, tile_rows, tile_cols)
    summed_one, summed_two = reduce_weights((grad_one, grad_two))
    return (input_grad, summed_one, summed_two)


def solution(mesh):
    placed = (P(None, "row", "col"), P(None, "row", "col"), P(), P(), P())
    return jax.shard_map(
        block,
        mesh=mesh,
        in_specs=placed,
        out_specs=(P(None, "row", "col"), P(("row", "col")), P(("row", "col"))),
        check_vma=False,
    )
```

```python
import jax
import jax.numpy as jnp
from jax import lax
from jax.sharding import PartitionSpec as P


def padded_2(cells, sides, width):
    for axis, dim in sides:
        count = lax.axis_size(axis)
        ends = count - 1
        head = lax.slice_in_dim(cells, 0, width, axis=dim)
        tail = lax.slice_in_dim(cells, cells.shape[dim] - width, cells.shape[dim], axis=dim)
        cells = jnp.concatenate(
            [
                lax.ppermute(tail, axis, [(i, (i + 1) % count) for i in range(ends)]),
                cells,
                lax.ppermute(head, axis, [((i + 1) % count, i) for i in range(ends)]),
            ],
            axis=dim,
        )
    return cells


def padded_pair(first, second, width):
    count = lax.axis_size("row")
    ends = count - 1
    rows = first.shape[1]
    head = jnp.concatenate([first[:, :width], second[:, :width]], axis=0)
    tail = jnp.concatenate([first[:, rows - width :], second[:, rows - width :]], axis=0)
    return jnp.concatenate(
        [
            lax.ppermute(tail, "row", [(i, (i + 1) % count) for i in range(ends)]),
            jnp.concatenate([first, second], axis=0),
            lax.ppermute(head, "row", [((i + 1) % count, i) for i in range(ends)]),
        ],
        axis=1,
    )


def window(padded, start_y, start_x, tile_rows, tile_cols):
    channels = padded.shape[0]
    piece = lax.slice(
        padded, (0, start_y, start_x), (channels, start_y + tile_rows, start_x + tile_cols)
    )
    return piece.reshape(channels, tile_rows * tile_cols)


def backward_taps(padded, kernel, other, tile_rows, tile_cols):
    channels = padded.shape[0]
    total = jnp.zeros((channels, tile_rows * tile_cols), jnp.float32)
    grads = []
    for offset_y in range(3):
        for offset_x in range(3):
            patch = window(padded, 2 - offset_y, 2 - offset_x, tile_rows, tile_cols)
            total = total + lax.dot_general(
                kernel[offset_y, offset_x],
                patch,
                (((0,), (0,)), ((), ())),
                preferred_element_type=jnp.float32,
            )
            grads.append(
                lax.dot_general(
                    patch, other, (((1,), (1,)), ((), ())), preferred_element_type=jnp.float32
                )
            )
    return (total, jnp.stack(grads).reshape(-1))


def reduce_weights(grads):
    rows, cols = lax.axis_size("row"), lax.axis_size("col")
    stacked = jnp.stack(grads).reshape(len(grads), rows, cols, -1)
    stacked = lax.all_to_all(stacked, "col", 2, 2, tiled=True).sum(axis=2)
    summed = lax.all_to_all(stacked, "row", 1, 1, tiled=True).sum(axis=1)
    return (summed[0], summed[1])


def local(features, cotangent, weight_one, bias_one, weight_two):
    channels, tile_rows, tile_cols = features.shape
    cell_count = tile_rows * tile_cols
    scale = float(cell_count * lax.axis_size("row") * lax.axis_size("col")) ** (-0.5)
    padded_both = padded_2(padded_pair(features, cotangent, 1), (("col", 2),), 1)
    padded_input, padded_cot = padded_both[:channels], padded_both[channels:]
    hidden = jnp.zeros((channels, cell_count), jnp.float32)
    for offset_y in range(3):
        for offset_x in range(3):
            patch = window(padded_input, offset_y, offset_x, tile_rows, tile_cols)
            hidden = hidden + jnp.dot(
                weight_one[offset_y, offset_x], patch, preferred_element_type=jnp.float32
            )
    hidden = hidden + bias_one[:, None]
    act = jax.nn.silu(hidden).astype(jnp.bfloat16)
    act_grad, grad_two = backward_taps(padded_cot, weight_two, act, tile_rows, tile_cols)
    grad_two = grad_two * scale
    sig = jax.nn.sigmoid(hidden)
    hidden_grad = (act_grad * sig * (1.0 + hidden * (1.0 - sig))).astype(jnp.bfloat16)
    padded_hid = padded_2(
        hidden_grad.reshape(channels, tile_rows, tile_cols), (("row", 1), ("col", 2)), 1
    )
    back_input, grad_one = backward_taps(
        padded_hid, weight_one, features.reshape(channels, cell_count), tile_rows, tile_cols
    )
    grad_one = grad_one * scale
    input_grad = (cotangent.reshape(channels, cell_count).astype(jnp.float32) + back_input).astype(
        jnp.bfloat16
    )
    input_grad = input_grad.reshape(channels, tile_rows, tile_cols)
    summed_one, summed_two = reduce_weights((grad_one, grad_two))
    return (input_grad, summed_one, summed_two)


def solution(mesh):
    placed = (P(None, "row", "col"), P(None, "row", "col"), P(), P(), P())
    return jax.shard_map(
        local,
        mesh=mesh,
        in_specs=placed,
        out_specs=(P(None, "row", "col"), P(("row", "col")), P(("row", "col"))),
        check_vma=False,
    )
```

```python
import jax
import jax.numpy as jnp
from jax import lax
from jax.sharding import PartitionSpec as P


def padded_2(cells, sides, width):
    for axis, dim in sides:
        count = lax.axis_size(axis)
        ends = count - 1
        head = lax.slice_in_dim(cells, 0, width, axis=dim)
        tail = lax.slice_in_dim(cells, cells.shape[dim] - width, cells.shape[dim], axis=dim)
        cells = jnp.concatenate(
            [
                lax.ppermute(tail, axis, [(i, (i + 1) % count) for i in range(ends)]),
                cells,
                lax.ppermute(head, axis, [((i + 1) % count, i) for i in range(ends)]),
            ],
            axis=dim,
        )
    return cells


def window(padded, start_y, start_x, tile_rows, tile_cols):
    channels = padded.shape[0]
    piece = lax.slice(
        padded, (0, start_y, start_x), (channels, start_y + tile_rows, start_x + tile_cols)
    )
    return piece.reshape(channels, tile_rows * tile_cols)


def backward_taps(padded, kernel, other, tile_rows, tile_cols):
    channels = padded.shape[0]
    total = jnp.zeros((channels, tile_rows * tile_cols), jnp.float32)
    grads = []
    for offset_y in range(3):
        for offset_x in range(3):
            patch = window(padded, 2 - offset_y, 2 - offset_x, tile_rows, tile_cols)
            total = total + lax.dot_general(
                kernel[offset_y, offset_x],
                patch,
                (((0,), (0,)), ((), ())),
                preferred_element_type=jnp.float32,
            )
            grads.append(
                lax.dot_general(
                    patch, other, (((1,), (1,)), ((), ())), preferred_element_type=jnp.float32
                )
            )
    return (total, jnp.stack(grads).reshape(-1))


def grad_taps(upper, padded, tile_rows, tile_cols):
    return jnp.stack(
        [
            lax.dot_general(
                upper,
                window(padded, offset_y, offset_x, tile_rows, tile_cols),
                (((1,), (1,)), ((), ())),
                preferred_element_type=jnp.float32,
            )
            for offset_y in range(3)
            for offset_x in range(3)
        ]
    ).reshape(-1)


def reduce_weights(grads):
    rows, cols = lax.axis_size("row"), lax.axis_size("col")
    stacked = jnp.stack(grads).reshape(len(grads), rows, cols, -1)
    stacked = lax.all_to_all(stacked, "col", 2, 2, tiled=True)
    stacked = stacked.sum(axis=2)
    summed = lax.all_to_all(stacked, "row", 1, 1, tiled=True).sum(axis=1)
    return (summed[0], summed[1])


def block(features, cotangent, weight_one, bias_one, weight_two):
    channels, tile_rows, tile_cols = features.shape
    cell_count = tile_rows * tile_cols
    scale = float(cell_count * lax.axis_size("row") * lax.axis_size("col")) ** (-0.5)
    padded_both = padded_2(
        jnp.concatenate([features, cotangent], axis=0), (("row", 1), ("col", 2)), 1
    )
    padded_input, padded_cot = padded_both[:channels], padded_both[channels:]
    hidden = jnp.zeros((channels, cell_count), jnp.float32)
    for offset_y in range(3):
        for offset_x in range(3):
            patch = window(padded_input, offset_y, offset_x, tile_rows, tile_cols)
            hidden = hidden + jnp.dot(
                weight_one[offset_y, offset_x], patch, preferred_element_type=jnp.float32
            )
    hidden = hidden + bias_one[:, None]
    act = jax.nn.silu(hidden).astype(jnp.bfloat16)
    act_grad, grad_two = backward_taps(padded_cot, weight_two, act, tile_rows, tile_cols)
    grad_two = grad_two * scale
    sig = jax.nn.sigmoid(hidden)
    hidden_grad = (act_grad * sig * (1.0 + hidden * (1.0 - sig))).astype(jnp.bfloat16)
    padded_hid = padded_2(hidden_grad.reshape(channels, tile_rows, tile_cols), (("row", 1),), 1)
    padded_hid = padded_2(padded_hid, (("col", 2),), 1)
    inner_grad = hidden_grad.reshape(channels, cell_count)
    grad_one = grad_taps(inner_grad, padded_input, tile_rows, tile_cols) * scale
    back_input, _ = backward_taps(padded_hid, weight_one, inner_grad, tile_rows, tile_cols)
    input_grad = (cotangent.reshape(channels, cell_count).astype(jnp.float32) + back_input).astype(
        jnp.bfloat16
    )
    input_grad = input_grad.reshape(channels, tile_rows, tile_cols)
    summed_one, summed_two = reduce_weights((grad_one, grad_two))
    return (input_grad, summed_one, summed_two)


def solution(mesh):
    placed = (P(None, "row", "col"), P(None, "row", "col"), P(), P(), P())
    return jax.shard_map(
        block,
        mesh=mesh,
        in_specs=placed,
        out_specs=(P(None, "row", "col"), P(("row", "col")), P(("row", "col"))),
        check_vma=False,
    )
```

```python
import jax
import jax.numpy as jnp
from jax import lax
from jax.sharding import PartitionSpec as P


def padded_2(cells, sides, width):
    for axis, dim in sides:
        count = lax.axis_size(axis)
        ends = count - 1
        head = lax.slice_in_dim(cells, 0, width, axis=dim)
        tail = lax.slice_in_dim(cells, cells.shape[dim] - width, cells.shape[dim], axis=dim)
        before = lax.ppermute(tail, axis, [(i, (i + 1) % count) for i in range(ends)])
        after = lax.ppermute(head, axis, [((i + 1) % count, i) for i in range(ends)])
        if dim == cells.ndim - 1 and width == 1:
            spread = [(0, 0)] * dim + [(1, 1)]
            lane = lax.broadcasted_iota(jnp.int32, (cells.shape[dim] + 2,), 0)
            cells = jnp.where(
                lane == 0,
                before,
                jnp.where(lane == cells.shape[dim] + 1, after, jnp.pad(cells, spread)),
            )
        else:
            cells = jnp.concatenate([before, cells, after], axis=dim)
    return cells


def window(padded, start_y, start_x, tile_rows, tile_cols):
    channels = padded.shape[0]
    piece = lax.slice(
        padded, (0, start_y, start_x), (channels, start_y + tile_rows, start_x + tile_cols)
    )
    return piece.reshape(channels, tile_rows * tile_cols)


def backward_taps(padded, kernel, other, tile_rows, tile_cols):
    channels = padded.shape[0]
    total = jnp.zeros((channels, tile_rows * tile_cols), jnp.float32)
    grads = []
    for offset_y in range(3):
        for offset_x in range(3):
            patch = window(padded, 2 - offset_y, 2 - offset_x, tile_rows, tile_cols)
            total = total + lax.dot_general(
                kernel[offset_y, offset_x],
                patch,
                (((0,), (0,)), ((), ())),
                preferred_element_type=jnp.float32,
            )
            grads.append(
                lax.dot_general(
                    patch, other, (((1,), (1,)), ((), ())), preferred_element_type=jnp.float32
                )
            )
    return (total, jnp.stack(grads).reshape(-1))


def reduce_weights(grads):
    rows, cols = lax.axis_size("row"), lax.axis_size("col")
    stacked = jnp.stack(grads).reshape(len(grads), rows, cols, -1)
    stacked = lax.all_to_all(stacked, "col", 2, 2, tiled=True).sum(axis=2)
    summed = lax.all_to_all(stacked, "row", 1, 1, tiled=True).sum(axis=1)
    return (summed[0], summed[1])


def local(features, cotangent, weight_one, bias_one, weight_two):
    channels, tile_rows, tile_cols = features.shape
    cell_count = tile_rows * tile_cols
    scale = float(cell_count * lax.axis_size("row") * lax.axis_size("col")) ** (-0.5)
    padded_both = padded_2(
        jnp.concatenate([features, cotangent], axis=0), (("row", 1), ("col", 2)), 1
    )
    padded_input, padded_cot = padded_both[:channels], padded_both[channels:]
    hidden = jnp.zeros((channels, cell_count), jnp.float32)
    for offset_y in range(3):
        for offset_x in range(3):
            patch = window(padded_input, offset_y, offset_x, tile_rows, tile_cols)
            hidden = hidden + jnp.dot(
                weight_one[offset_y, offset_x], patch, preferred_element_type=jnp.float32
            )
    hidden = hidden + bias_one[:, None]
    act = jax.nn.silu(hidden).astype(jnp.bfloat16)
    act_grad, grad_two = backward_taps(padded_cot, weight_two, act, tile_rows, tile_cols)
    grad_two = grad_two * scale
    sig = jax.nn.sigmoid(hidden)
    hidden_grad = (act_grad * sig * (1.0 + hidden * (1.0 - sig))).astype(jnp.bfloat16)
    padded_hid = padded_2(
        hidden_grad.reshape(channels, tile_rows, tile_cols), (("row", 1), ("col", 2)), 1
    )
    back_input, grad_one = backward_taps(
        padded_hid, weight_one, features.reshape(channels, cell_count), tile_rows, tile_cols
    )
    grad_one = grad_one * scale
    input_grad = (cotangent.reshape(channels, cell_count).astype(jnp.float32) + back_input).astype(
        jnp.bfloat16
    )
    input_grad = input_grad.reshape(channels, tile_rows, tile_cols)
    summed_one, summed_two = reduce_weights((grad_one, grad_two))
    return (input_grad, summed_one, summed_two)


def solution(mesh):
    placed = (P(None, "row", "col"), P(None, "row", "col"), P(), P(), P())
    return jax.shard_map(
        local,
        mesh=mesh,
        in_specs=placed,
        out_specs=(P(None, "row", "col"), P(("row", "col")), P(("row", "col"))),
        check_vma=False,
    )
```

```python
import jax
import jax.numpy as jnp
from jax import lax
from jax.sharding import PartitionSpec as P


def padded_2(cells, sides, width):
    for axis, dim in sides:
        count = lax.axis_size(axis)
        ends = count - 1
        head = lax.slice_in_dim(cells, 0, width, axis=dim)
        tail = lax.slice_in_dim(cells, cells.shape[dim] - width, cells.shape[dim], axis=dim)
        before = lax.ppermute(tail, axis, [(i, (i + 1) % count) for i in range(ends)])
        after = lax.ppermute(head, axis, [((i + 1) % count, i) for i in range(ends)])
        if dim == cells.ndim - 1 and width == 1:
            spread = [(0, 0)] * dim + [(1, 1)]
            lane = lax.broadcasted_iota(jnp.int32, (cells.shape[dim] + 2,), 0)
            cells = jnp.where(
                lane == 0,
                before,
                jnp.where(lane == cells.shape[dim] + 1, after, jnp.pad(cells, spread)),
            )
        else:
            cells = jnp.concatenate([before, cells, after], axis=dim)
    return cells


def window(padded, start_y, start_x, tile_rows, tile_cols):
    channels = padded.shape[0]
    piece = lax.slice(
        padded, (0, start_y, start_x), (channels, start_y + tile_rows, start_x + tile_cols)
    )
    return piece.reshape(channels, tile_rows * tile_cols)


def backward_taps(padded, kernel, other, tile_rows, tile_cols):
    channels = padded.shape[0]
    total = jnp.zeros((channels, tile_rows * tile_cols), jnp.float32)
    grads = []
    for offset_y in range(3):
        for offset_x in range(3):
            patch = window(padded, 2 - offset_y, 2 - offset_x, tile_rows, tile_cols)
            total = total + lax.dot_general(
                kernel[offset_y, offset_x],
                patch,
                (((0,), (0,)), ((), ())),
                preferred_element_type=jnp.float32,
            )
            grads.append(
                lax.dot_general(
                    patch, other, (((1,), (1,)), ((), ())), preferred_element_type=jnp.float32
                )
            )
    return (total, jnp.stack(grads).reshape(-1))


def reduce_weights(grads):
    rows, cols = lax.axis_size("row"), lax.axis_size("col")
    stacked = jnp.stack(grads).reshape(len(grads), rows, cols, -1)
    stacked = lax.all_to_all(stacked, "col", 2, 2, tiled=True).sum(axis=2)
    summed = lax.all_to_all(stacked, "row", 1, 1, tiled=True).sum(axis=1)
    return (summed[0], summed[1])


def local(features, cotangent, weight_one, bias_one, weight_two):
    channels, tile_rows, tile_cols = features.shape
    cell_count = tile_rows * tile_cols
    scale = float(cell_count * lax.axis_size("row") * lax.axis_size("col")) ** (-0.5)
    padded_both = padded_2(
        jnp.concatenate([features, cotangent], axis=0), (("row", 1), ("col", 2)), 1
    )
    padded_input, padded_cot = padded_both[:channels], padded_both[channels:]
    hidden = jnp.zeros((channels, cell_count), jnp.float32)
    for offset_y in range(3):
        for offset_x in range(3):
            patch = window(padded_input, offset_y, offset_x, tile_rows, tile_cols)
            hidden = hidden + jnp.dot(
                weight_one[offset_y, offset_x], patch, preferred_element_type=jnp.float32
            )
    hidden = hidden + bias_one[:, None]
    act = jax.nn.silu(hidden).astype(jnp.bfloat16)
    act_grad, grad_two = backward_taps(padded_cot, weight_two, act, tile_rows, tile_cols)
    sig = jax.nn.sigmoid(hidden)
    hidden_grad = (act_grad * sig * (1.0 + hidden * (1.0 - sig))).astype(jnp.bfloat16)
    padded_hid = padded_2(
        hidden_grad.reshape(channels, tile_rows, tile_cols), (("row", 1), ("col", 2)), 1
    )
    back_input, grad_one = backward_taps(
        padded_hid, weight_one, features.reshape(channels, cell_count), tile_rows, tile_cols
    )
    input_grad = (cotangent.reshape(channels, cell_count).astype(jnp.float32) + back_input).astype(
        jnp.bfloat16
    )
    input_grad = input_grad.reshape(channels, tile_rows, tile_cols)
    summed_one, summed_two = reduce_weights((grad_one, grad_two))
    summed_one, summed_two = summed_one * scale, summed_two * scale
    return (input_grad, summed_one, summed_two)


def solution(mesh):
    placed = (P(None, "row", "col"), P(None, "row", "col"), P(), P(), P())
    return jax.shard_map(
        local,
        mesh=mesh,
        in_specs=placed,
        out_specs=(P(None, "row", "col"), P(("row", "col")), P(("row", "col"))),
        check_vma=False,
    )
```

```python
import jax
import jax.numpy as jnp
from jax import lax
from jax.sharding import PartitionSpec as P


def padded_2(cells, sides, width):
    for axis, dim in sides:
        count = lax.axis_size(axis)
        ends = count - 1
        head = lax.slice_in_dim(cells, 0, width, axis=dim)
        tail = lax.slice_in_dim(cells, cells.shape[dim] - width, cells.shape[dim], axis=dim)
        before = lax.ppermute(tail, axis, [(i, (i + 1) % count) for i in range(ends)])
        after = lax.ppermute(head, axis, [((i + 1) % count, i) for i in range(ends)])
        if width == 1:
            spread = [(0, 0)] * dim + [(1, 1)] + [(0, 0)] * (cells.ndim - 1 - dim)
            shape = [1] * cells.ndim
            shape[dim] = cells.shape[dim] + 2
            lane = lax.broadcasted_iota(jnp.int32, tuple(shape), dim)
            cells = jnp.where(
                lane == 0,
                before,
                jnp.where(lane == cells.shape[dim] + 1, after, jnp.pad(cells, spread)),
            )
        else:
            cells = jnp.concatenate([before, cells, after], axis=dim)
    return cells


def window(padded, start_y, start_x, tile_rows, tile_cols):
    channels = padded.shape[0]
    piece = lax.slice(
        padded, (0, start_y, start_x), (channels, start_y + tile_rows, start_x + tile_cols)
    )
    return piece.reshape(channels, tile_rows * tile_cols)


def backward_taps(padded, kernel, other, tile_rows, tile_cols):
    channels = padded.shape[0]
    total = jnp.zeros((channels, tile_rows * tile_cols), jnp.float32)
    grads = []
    for offset_y in range(3):
        for offset_x in range(3):
            patch = window(padded, 2 - offset_y, 2 - offset_x, tile_rows, tile_cols)
            total = total + lax.dot_general(
                kernel[offset_y, offset_x],
                patch,
                (((0,), (0,)), ((), ())),
                preferred_element_type=jnp.float32,
            )
            grads.append(
                lax.dot_general(
                    patch, other, (((1,), (1,)), ((), ())), preferred_element_type=jnp.float32
                )
            )
    return (total, jnp.stack(grads).reshape(-1))


def reduce_weights(grads):
    rows, cols = lax.axis_size("row"), lax.axis_size("col")
    stacked = jnp.stack(grads).reshape(len(grads), rows, cols, -1)
    stacked = lax.all_to_all(stacked, "col", 2, 2, tiled=True).sum(axis=2)
    summed = lax.all_to_all(stacked, "row", 1, 1, tiled=True).sum(axis=1)
    return (summed[0], summed[1])


def local(features, cotangent, weight_one, bias_one, weight_two):
    channels, tile_rows, tile_cols = features.shape
    cell_count = tile_rows * tile_cols
    scale = float(cell_count * lax.axis_size("row") * lax.axis_size("col")) ** (-0.5)
    padded_both = padded_2(
        jnp.concatenate([features, cotangent], axis=0), (("row", 1), ("col", 2)), 1
    )
    padded_input, padded_cot = padded_both[:channels], padded_both[channels:]
    hidden = jnp.zeros((channels, cell_count), jnp.float32)
    for offset_y in range(3):
        for offset_x in range(3):
            patch = window(padded_input, offset_y, offset_x, tile_rows, tile_cols)
            hidden = hidden + jnp.dot(
                weight_one[offset_y, offset_x], patch, preferred_element_type=jnp.float32
            )
    hidden = hidden + bias_one[:, None]
    act = jax.nn.silu(hidden).astype(jnp.bfloat16)
    act_grad, grad_two = backward_taps(padded_cot, weight_two, act, tile_rows, tile_cols)
    grad_two = grad_two * scale
    sig = jax.nn.sigmoid(hidden)
    hidden_grad = (act_grad * sig * (1.0 + hidden * (1.0 - sig))).astype(jnp.bfloat16)
    padded_hid = padded_2(
        hidden_grad.reshape(channels, tile_rows, tile_cols), (("row", 1), ("col", 2)), 1
    )
    back_input, grad_one = backward_taps(
        padded_hid, weight_one, features.reshape(channels, cell_count), tile_rows, tile_cols
    )
    grad_one = grad_one * scale
    input_grad = (cotangent.reshape(channels, cell_count).astype(jnp.float32) + back_input).astype(
        jnp.bfloat16
    )
    input_grad = input_grad.reshape(channels, tile_rows, tile_cols)
    summed_one, summed_two = reduce_weights((grad_one, grad_two))
    return (input_grad, summed_one, summed_two)


def solution(mesh):
    placed = (P(None, "row", "col"), P(None, "row", "col"), P(), P(), P())
    return jax.shard_map(
        local,
        mesh=mesh,
        in_specs=placed,
        out_specs=(P(None, "row", "col"), P(("row", "col")), P(("row", "col"))),
        check_vma=False,
    )
```
